32 devices in a mesh: dp: 4 (over y, core), ctx: 2 (over x), tensor: 4 (over z).
Axes of the slice: x: 2, y: 2, z: 4, core: 2. Of those that a mesh axis runs over, the one named last changes fastest.
Arguments:
- inputs: bfloat16 [4, 1024, 768], P('dp', 'ctx'), may hold values from -6 to 6
- encoded: bfloat16 [4, 512, 768], P('dp', 'ctx'), may hold values from -6 to 6
- seq_len: int32 [4], P('dp'), may hold values from 128 to 1024, as said below
- enc_len: int32 [4], P('dp'), may hold values from 64 to 512, as said below
- norm_self: bfloat16 [768], P(('dp', 'ctx')), may hold values from 0.25 to 1.75
- w_query: bfloat16 [768, 768], P(('dp', 'ctx'), 'tensor'), may hold values from -0.02734375 to 0.02734375
- w_key: bfloat16 [768, 768], P(('dp', 'ctx'), 'tensor'), may hold values from -0.21875 to 0.21875
- w_value: bfloat16 [768, 768], P(('dp', 'ctx'), 'tensor'), may hold values from -0.21875 to 0.21875
- w_out: bfloat16 [768, 768], P('tensor', ('dp', 'ctx')), may hold values from -1.75 to 1.75
- rel_table: float32 [32, 12], P(None, 'tensor'), may hold values from -4 to 4
- norm_cross: bfloat16 [768], P(('dp', 'ctx')), may hold values from 0.25 to 1.75
- c_query: bfloat16 [768, 768], P(('dp', 'ctx'), 'tensor'), may hold values from -0.02734375 to 0.02734375
- c_key: bfloat16 [768, 768], P(('dp', 'ctx'), 'tensor'), may hold values from -0.21875 to 0.21875
- c_value: bfloat16 [768, 768], P(('dp', 'ctx'), 'tensor'), may hold values from -0.21875 to 0.21875
- c_out: bfloat16 [768, 768], P('tensor', ('dp', 'ctx')), may hold values from -1.25 to 1.25
- norm_ff: bfloat16 [768], P(('dp', 'ctx')), may hold values from 0.25 to 1.75
- w_gate: bfloat16 [768, 2048], P(('dp', 'ctx'), 'tensor'), may hold values from -0.21875 to 0.21875
- w_up: bfloat16 [768, 2048], P(('dp', 'ctx'), 'tensor'), may hold values from -0.21875 to 0.21875
- w_down: bfloat16 [2048, 768], P('tensor', ('dp', 'ctx')), may hold values from -0.125 to 0.125
- cotangent: bfloat16 [4, 1024, 768], P('dp', 'ctx'), may hold values from -6 to 6
Outputs:
- layer_out: bfloat16 [4, 1024, 768], P('dp', 'ctx')
- grad_inputs: float32 [4, 1024, 768], P('dp', 'ctx')
- grad_encoded: float32 [4, 512, 768], P('dp', 'ctx')
- grad_norm_self: float32 [768], P(('dp', 'ctx'))
- grad_w_query: float32 [768, 768], P(('dp', 'ctx'), 'tensor')
- grad_w_key: float32 [768, 768], P(('dp', 'ctx'), 'tensor')
- grad_w_value: float32 [768, 768], P(('dp', 'ctx'), 'tensor')
- grad_w_out: float32 [768, 768], P('tensor', ('dp', 'ctx'))
- grad_rel_table: float32 [32, 12], P(None, 'tensor')
- grad_norm_cross: float32 [768], P(('dp', 'ctx'))
- grad_c_query: float32 [768, 768], P(('dp', 'ctx'), 'tensor')
- grad_c_key: float32 [768, 768], P(('dp', 'ctx'), 'tensor')
- grad_c_value: float32 [768, 768], P(('dp', 'ctx'), 'tensor')
- grad_c_out: float32 [768, 768], P('tensor', ('dp', 'ctx'))
- grad_norm_ff: float32 [768], P(('dp', 'ctx'))
- grad_w_gate: float32 [768, 2048], P(('dp', 'ctx'), 'tensor')
- grad_w_up: float32 [768, 2048], P(('dp', 'ctx'), 'tensor')
- grad_w_down: float32 [2048, 768], P('tensor', ('dp', 'ctx'))
The draws below stay inside these ranges and needn't reach their ends.
Inputs may be any that keep to these rules, and one draw needn't show every extreme that they name: `seq_len`: live tokens of each sequence; in every draw some sequence has 1024 and some has 128. `enc_len`: live encoder states of each sequence; in every draw some sequence has 512 and some has 64.
All inputs are finite; a program needn't handle non-finite values.
Results may differ from the reference program's by a relative error of at most 0.018.
Values may be sent and summed in bfloat16 or wider, within the bound.
No kernel may reach another device: no remote copies, remote signals or barrier semaphores. Data moves between devices by JAX's collectives and lax.ppermute only.
A program may use at most 128 MiB of HBM per device.

```python
import math
import jax
import jax.numpy as jnp
from jax import lax

D = 768
H = 12
HD = 64
FF = 2048
BUCKETS = 32
L = 1024
E = 512
DSEQ = 4


def live_lengths(key, longest):
    first, second = jax.random.split(key)
    drawn = jax.random.randint(first, (DSEQ,), longest // 8, longest + 1, dtype=jnp.int32)
    order = jax.random.permutation(second, DSEQ)
    return drawn.at[order[0]].set(longest).at[order[1]].set(longest // 8).astype(jnp.int32)


def draw_seq_len(key, part):
    return live_lengths(jax.random.fold_in(key, 11), L)


def draw_enc_len(key, part):
    return live_lengths(jax.random.fold_in(key, 23), E)


def block_levels(stream_key, extent, pieces, least, top_value):
    loudness, own = 1.0, jax.random.fold_in(stream_key, 6)
    for dim, blocks in pieces:
        draws = jnp.exp(jax.random.uniform(jax.random.fold_in(own, dim), (blocks,), jnp.float32, least / len(pieces), top_value / len(pieces)))
        loudness = loudness * jnp.repeat(draws, extent[dim] // blocks).reshape([-1 if axis == dim else 1 for axis in range(len(extent))])
    return loudness


def bell_draw(own_key, extent, spread, limit, cuts=(), kind=jnp.bfloat16):
    level = block_levels(own_key, extent, cuts, -0.22, 0.18) if cuts else 1.0
    entries = jax.random.normal(own_key, extent, jnp.float32) * spread * level
    return jnp.minimum(jnp.maximum(entries, -limit), limit).astype(kind)


def setup_inputs(seed: int = 0) -> dict:
    streams_of = jax.random.split(jax.random.key(seed), 21)
    return {
        "inputs": bell_draw(streams_of[0], (DSEQ, L, D), 1.0, 6.0, ((0, 4), (1, 2))),
        "encoded": bell_draw(streams_of[1], (DSEQ, E, D), 1.0, 6.0, ((0, 4), (1, 2))),
        "seq_len": draw_seq_len(jax.random.fold_in(streams_of[20], 71), 0),
        "enc_len": draw_enc_len(jax.random.fold_in(streams_of[20], 71), 0),
        "norm_self": jnp.clip(1.0 + 0.15 * jax.random.normal(streams_of[4], (D,), jnp.float32), 0.25, 1.75).astype(jnp.bfloat16),
        "w_query": bell_draw(streams_of[5], (D, H * HD), (D * HD) ** -0.5, 0.02734375, ((0, 8), (1, 4))),
        "w_key": bell_draw(streams_of[6], (D, H * HD), D ** -0.5, 0.21875, ((0, 8), (1, 4))),
        "w_value": bell_draw(streams_of[7], (D, H * HD), D ** -0.5, 0.21875, ((0, 8), (1, 4))),
        "w_out": bell_draw(streams_of[8], (H * HD, D), (max(H * HD * 16 // L, 1)) ** -0.5, 1.75, ((0, 4), (1, 8))),
        "rel_table": bell_draw(streams_of[9], (BUCKETS, H), 1.0, 4.0, ((1, 4),), jnp.float32),
        "norm_cross": jnp.clip(1.0 + 0.15 * jax.random.normal(streams_of[10], (D,), jnp.float32), 0.25, 1.75).astype(jnp.bfloat16),
        "c_query": bell_draw(streams_of[11], (D, H * HD), (D * HD) ** -0.5, 0.02734375, ((0, 8), (1, 4))),
        "c_key": bell_draw(streams_of[12], (D, H * HD), D ** -0.5, 0.21875, ((0, 8), (1, 4))),
        "c_value": bell_draw(streams_of[13], (D, H * HD), D ** -0.5, 0.21875, ((0, 8), (1, 4))),
        "c_out": bell_draw(streams_of[14], (H * HD, D), (max(H * HD * 16 // E, 1)) ** -0.5, 1.25, ((0, 4), (1, 8))),
        "norm_ff": jnp.clip(1.0 + 0.15 * jax.random.normal(streams_of[15], (D,), jnp.float32), 0.25, 1.75).astype(jnp.bfloat16),
        "w_gate": bell_draw(streams_of[16], (D, FF), D ** -0.5, 0.21875, ((0, 8), (1, 4))),
        "w_up": bell_draw(streams_of[17], (D, FF), D ** -0.5, 0.21875, ((0, 8), (1, 4))),
        "w_down": bell_draw(streams_of[18], (FF, D), FF ** -0.5, 0.125, ((0, 4), (1, 8))),
        "cotangent": bell_draw(streams_of[19], (DSEQ, L, D), 1.0, 6.0, ((0, 4), (1, 2))),
    }


bucket_edges = list(range(1, 17)) + [math.ceil(16.0 * 8.0 ** ((bucket_index - 16) / 16.0)) for bucket_index in range(17, 32)]

def rounded(values):
    return lax.optimization_barrier(values.astype(jnp.bfloat16))

def bucket_of(distance):
    result = jnp.zeros(distance.shape, jnp.int32)
    for threshold in bucket_edges:
        result = result + (distance >= threshold).astype(jnp.int32)
    return result

def distance_table(bias_table, length):
    buckets = bucket_of(jnp.arange(length, dtype=jnp.int32))
    result = jnp.zeros((bias_table.shape[1], length), jnp.float32)
    for bucket in range(bias_table.shape[0]):
        result = jnp.where(buckets[None, :] == bucket, bias_table[bucket][:, None], result)
    return result

def table_grad(per_distance, count):
    buckets = bucket_of(jnp.arange(per_distance.shape[1], dtype=jnp.int32))
    return jnp.stack([lax.optimization_barrier(jnp.sum(jnp.where(buckets[None, :] == bucket, per_distance, 0.0), axis=1)) for bucket in range(count)])

def distance_sums(score_sum, distance, length):
    flat_ids = distance.reshape(-1)

    def one_head(plane):
        return jax.ops.segment_sum(plane.reshape(-1), flat_ids, num_segments=length)
    return jax.vmap(one_head)(score_sum)

def rms_norm(hidden, norm_gain):
    rescale = lax.rsqrt(lax.optimization_barrier(jnp.mean(hidden * hidden, axis=-1, keepdims=True)) + 1e-06)
    normed = hidden * rescale
    return (normed, rescale, rounded(normed * norm_gain.astype(jnp.float32)))

def norm_back(grad_in, normed, rescale, norm_gain):
    grad_scaled = grad_in * norm_gain.astype(jnp.float32)
    grad_hidden = rescale * (grad_scaled - normed * lax.optimization_barrier(jnp.mean(grad_scaled * normed, axis=-1, keepdims=True)))
    grad_gain = lax.optimization_barrier(jnp.sum((grad_in * normed).reshape(-1, normed.shape[-1]), axis=0))
    return (grad_hidden, grad_gain)

def gelu_parts(preact):
    argument = 0.7978845608028654 * (preact + 0.044715 * preact * preact * preact)
    tangent = jnp.tanh(argument)
    gelu_value = 0.5 * preact * (1.0 + tangent)
    gelu_slope = 0.5 * (1.0 + tangent) + 0.5 * preact * (1.0 - tangent * tangent) * 0.7978845608028654 * (1.0 + 3.0 * 0.044715 * preact * preact)
    return (gelu_value, gelu_slope)

def masked_scores(queries, key_rows, bias, allowed):
    scores = jnp.einsum('rhd,khd->hrk', queries.astype(jnp.float32), key_rows.astype(jnp.float32)) + bias
    return jnp.where(allowed[None], scores, -1e+30)

def attend(queries, key_rows, values, bias, allowed):
    scores = masked_scores(queries, key_rows, bias, allowed)
    highest = lax.optimization_barrier(jnp.max(scores, axis=-1, keepdims=True))
    log_total = highest + jnp.log(lax.optimization_barrier(jnp.sum(jnp.exp(scores - highest), axis=-1, keepdims=True)))
    weights_b = rounded(jnp.exp(scores - log_total))
    output = jnp.einsum('hrk,khd->rhd', weights_b.astype(jnp.float32), values.astype(jnp.float32))
    return (rounded(output), log_total)

def attend_back(queries, key_rows, values, bias, allowed, log_total, grad_output):
    scores = masked_scores(queries, key_rows, bias, allowed)
    attn_prob = jnp.exp(scores - log_total)
    prob_b = rounded(attn_prob)
    grad_prob = jnp.einsum('rhd,khd->hrk', grad_output.astype(jnp.float32), values.astype(jnp.float32))
    row_dot = lax.optimization_barrier(jnp.sum(attn_prob * grad_prob, axis=-1, keepdims=True))
    grad_scores = attn_prob * (grad_prob - row_dot)
    scores_b = rounded(grad_scores).astype(jnp.float32)
    grad_query = rounded(jnp.einsum('hrk,khd->rhd', scores_b, key_rows.astype(jnp.float32)))
    grad_keys = jnp.einsum('hrk,rhd->khd', scores_b, queries.astype(jnp.float32))
    grad_values = jnp.einsum('hrk,rhd->khd', prob_b.astype(jnp.float32), grad_output.astype(jnp.float32))
    return (grad_query, grad_keys, grad_values, grad_scores)

def grouped_sum(products):
    row_count = products[0][0].shape[0]
    summed = jnp.zeros((row_count, products[0][1].shape[1]), jnp.float32)
    for operand, weight in products:
        summed = summed + jnp.dot(operand, weight, preferred_element_type=jnp.float32)
    return summed

def split_heads(matrix, count):
    return matrix.reshape(count, -1, H, HD)

def outer(operand, other):
    return jnp.dot(operand.T, other, preferred_element_type=jnp.float32)

def project(operand, weight):
    return rounded(jnp.dot(operand, weight, preferred_element_type=jnp.float32))

def reference(inputs, encoded, seq_len, enc_len, norm_self, w_query, w_key, w_value, w_out, rel_table, norm_cross, c_query, c_key, c_value, c_out, norm_ff, w_gate, w_up, w_down, cotangent):
    positions = jnp.arange(L, dtype=jnp.int32)
    enc_positions = jnp.arange(E, dtype=jnp.int32)
    distance = jnp.maximum(positions[:, None] - positions[None, :], 0)
    self_bias = jnp.take(distance_table(rel_table, L), distance, axis=1)
    causal = positions[None, :] <= positions[:, None]
    live_rows = (positions[None, :] < seq_len[:, None]).astype(jnp.float32).reshape(-1, 1)
    enc_flat = encoded.reshape(-1, D)

    def self_mask(length):
        return causal & (positions[None, :] < length)

    def cross_mask(length):
        return jnp.broadcast_to(enc_positions[None, :] < length, (L, E))
    hidden_in = inputs.astype(jnp.float32).reshape(-1, D)
    normed_one, rescale_one, input_one = rms_norm(hidden_in, norm_self)
    query_one = split_heads(project(input_one, w_query), DSEQ)
    key_one = split_heads(project(input_one, w_key), DSEQ)
    value_one = split_heads(project(input_one, w_value), DSEQ)

    def self_forward(members):
        queries, key_rows, values, length = members
        return attend(queries, key_rows, values, self_bias, self_mask(length))
    attn_one, total_one = lax.map(self_forward, (query_one, key_one, value_one, seq_len))
    flat_one = attn_one.reshape(-1, H * HD)
    hidden_one = hidden_in + grouped_sum(((flat_one, w_out),))
    normed_two, rescale_two, input_two = rms_norm(hidden_one, norm_cross)
    query_two = split_heads(project(input_two, c_query), DSEQ)
    key_two = split_heads(project(enc_flat, c_key), DSEQ)
    value_two = split_heads(project(enc_flat, c_value), DSEQ)

    def cross_forward(members):
        queries, key_rows, values, length = members
        return attend(queries, key_rows, values, 0.0, cross_mask(length))
    attn_two, total_two = lax.map(cross_forward, (query_two, key_two, value_two, enc_len))
    flat_two = attn_two.reshape(-1, H * HD)
    hidden_two = hidden_one + grouped_sum(((flat_two, c_out),))
    normed_three, rescale_three, input_three = rms_norm(hidden_two, norm_ff)
    gate_pre = jnp.dot(input_three, w_gate, preferred_element_type=jnp.float32)
    up_pre = jnp.dot(input_three, w_up, preferred_element_type=jnp.float32)
    gelu_value, gelu_slope = gelu_parts(gate_pre)
    ff_hidden = rounded(gelu_value * up_pre)
    layer_out = (hidden_two + grouped_sum(((ff_hidden, w_down),))).astype(jnp.bfloat16).reshape(DSEQ, L, D)
    grad_out = cotangent.astype(jnp.float32).reshape(-1, D) * live_rows
    grad_out_b = rounded(grad_out)
    grad_w_down = outer(ff_hidden, grad_out_b)
    grad_ff = jnp.dot(grad_out_b, w_down.T, preferred_element_type=jnp.float32)
    grad_gate = rounded(grad_ff * up_pre * gelu_slope)
    grad_up = rounded(grad_ff * gelu_value)
    grad_w_gate = outer(input_three, grad_gate)
    grad_w_up = outer(input_three, grad_up)
    grad_normed_three = grouped_sum(((grad_gate, w_gate.T), (grad_up, w_up.T)))
    back_three, grad_norm_ff = norm_back(grad_normed_three, normed_three, rescale_three, norm_ff)
    grad_two = grad_out + back_three
    grad_two_b = rounded(grad_two)
    grad_c_out = outer(flat_two, grad_two_b)
    grad_attn_two = split_heads(project(grad_two_b, c_out.T), DSEQ)

    def cross_backward(members):
        queries, key_rows, values, length, log_total, grad_output = members
        grad_query, grad_keys, grad_values, unused = attend_back(queries, key_rows, values, 0.0, cross_mask(length), log_total, grad_output)
        return (grad_query, grad_keys, grad_values)
    query_grad_two, key_grad_two, value_grad_two = lax.map(cross_backward, (query_two, key_two, value_two, enc_len, total_two, grad_attn_two))
    query_grad_two = query_grad_two.reshape(-1, H * HD)
    key_grad_two = rounded(key_grad_two.reshape(-1, H * HD))
    value_grad_two = rounded(value_grad_two.reshape(-1, H * HD))
    grad_c_query = outer(input_two, query_grad_two)
    grad_c_key = outer(enc_flat, key_grad_two)
    grad_c_value = outer(enc_flat, value_grad_two)
    grad_encoded = grouped_sum(((key_grad_two, c_key.T), (value_grad_two, c_value.T))).reshape(DSEQ, E, D)
    grad_normed_two = grouped_sum(((query_grad_two, c_query.T),))
    back_two, grad_norm_cross = norm_back(grad_normed_two, normed_two, rescale_two, norm_cross)
    grad_one = grad_two + back_two
    grad_one_b = rounded(grad_one)
    grad_w_out = outer(flat_one, grad_one_b)
    grad_attn_one = split_heads(project(grad_one_b, w_out.T), DSEQ)

    def self_backward(carry, members):
        queries, key_rows, values, length, log_total, grad_output = members
        grad_query, grad_keys, grad_values, grad_scores = attend_back(queries, key_rows, values, self_bias, self_mask(length), log_total, grad_output)
        return (carry + grad_scores, (grad_query, grad_keys, grad_values))
    score_sum, (query_grad_one, key_grad_one, value_grad_one) = lax.scan(self_backward, jnp.zeros((H, L, L), jnp.float32), (query_one, key_one, value_one, seq_len, total_one, grad_attn_one))
    grad_rel_table = table_grad(distance_sums(score_sum, distance, L), BUCKETS)
    query_grad_one = query_grad_one.reshape(-1, H * HD)
    key_grad_one = rounded(key_grad_one.reshape(-1, H * HD))
    value_grad_one = rounded(value_grad_one.reshape(-1, H * HD))
    grad_w_query = outer(input_one, query_grad_one)
    grad_w_key = outer(input_one, key_grad_one)
    grad_w_value = outer(input_one, value_grad_one)
    grad_normed_one = grouped_sum(((query_grad_one, w_query.T), (key_grad_one, w_key.T), (value_grad_one, w_value.T)))
    back_one, grad_norm_self = norm_back(grad_normed_one, normed_one, rescale_one, norm_self)
    grad_inputs = (grad_one + back_one).reshape(DSEQ, L, D)
    return (layer_out, grad_inputs, grad_encoded, grad_norm_self, grad_w_query, grad_w_key, grad_w_value, grad_w_out, grad_rel_table, grad_norm_cross, grad_c_query, grad_c_key, grad_c_value, grad_c_out, grad_norm_ff, grad_w_gate, grad_w_up, grad_w_down)
```

```python
import math

import jax
import jax.numpy as jnp
from jax import lax
from jax.experimental import pallas as pl
from jax.experimental.pallas import tpu as pltpu
from jax.sharding import PartitionSpec as P

bf16 = jnp.bfloat16
f32 = jnp.float32
MASKED = -1e30


bucket_edges = list(range(1, 17)) + [
    math.ceil(16.0 * 8.0 ** ((bucket_index - 16) / 16.0)) for bucket_index in range(17, 32)
]


def bucket_of(distance):
    result = jnp.zeros(distance.shape, jnp.int32)
    for threshold in bucket_edges:
        result = result + (distance >= threshold).astype(jnp.int32)
    return result


def dot(a, b):
    return lax.dot_general(a, b, (((1,), (0,)), ((), ())), preferred_element_type=f32)


def dot_nt(a, b):
    return lax.dot_general(a, b, (((1,), (1,)), ((), ())), preferred_element_type=f32)


def dot_tn(a, b):
    return lax.dot_general(a, b, (((0,), (0,)), ((), ())), preferred_element_type=f32)


def rms_norm(hidden, gain):
    rescale = lax.rsqrt(jnp.mean(hidden * hidden, axis=-1, keepdims=True) + 1e-06)
    normed = hidden * rescale
    return normed, rescale, (normed * gain).astype(bf16)


def norm_back(grad_in, normed, rescale, gain):
    grad_scaled = grad_in * gain
    return rescale * (grad_scaled - normed * jnp.mean(grad_scaled * normed, axis=-1, keepdims=True))


def gelu_parts(preact):
    argument = 0.7978845608028654 * (preact + 0.044715 * preact * preact * preact)
    tangent = jnp.tanh(argument)
    gelu_value = 0.5 * preact * (1.0 + tangent)
    gelu_slope = 0.5 * (1.0 + tangent) + 0.5 * preact * (
        1.0 - tangent * tangent
    ) * 0.7978845608028654 * (1.0 + 3.0 * 0.044715 * preact * preact)
    return gelu_value, gelu_slope


def bias_tiles(vectors, tile):
    heads, steps, width = vectors.shape

    def kernel(v_ref, out_ref):
        row = lax.broadcasted_iota(jnp.int32, (tile, tile), 0)
        col = lax.broadcasted_iota(jnp.int32, (tile, tile), 1)
        for step in range(steps):
            spread = jnp.broadcast_to(v_ref[0, step : step + 1, :], (tile, width))
            skewed = pltpu.roll(spread, 0, 1, stride=1, stride_axis=0)[:, :tile]
            if step == 0:
                skewed = jnp.where(col <= row, skewed, MASKED)
            out_ref[0, step] = skewed
        out_ref[0, steps] = jnp.full((tile, tile), MASKED, f32)

    return pl.pallas_call(
        kernel,
        grid=(heads,),
        in_specs=[pl.BlockSpec((1, steps, width), lambda h: (h, 0, 0))],
        out_specs=pl.BlockSpec((1, steps + 1, tile, tile), lambda h: (h, 0, 0, 0)),
        out_shape=jax.ShapeDtypeStruct((heads, steps + 1, tile, tile), f32),
        name="bias_tiles",
    )(vectors)


def tile_index(q_block, k_block, steps):
    delta = q_block - k_block
    return jnp.where(delta >= 0, delta, steps)


def attend(q, k, v, key_mask, head_count, tile, places=None, tiles=None):
    rows, width = q.shape
    keys = k.shape[0]
    head_width = width // head_count
    with_bias = tiles is not None
    blocks = keys // tile if with_bias else 0
    steps = tiles.shape[1] - 1 if with_bias else 0

    def kernel(*refs):
        if with_bias:
            qp_ref, kp_ref, q_ref, k_ref, v_ref, m_ref, b_ref, o_ref, lse_ref = refs
        else:
            q_ref, k_ref, v_ref, m_ref, o_ref, lse_ref = refs
        lane = lax.broadcasted_iota(jnp.int32, (1, width), 1)
        queries = q_ref[...]
        mask_row = m_ref[...]
        result = jnp.zeros((tile, width), f32)
        if with_bias:
            q_block = qp_ref[pl.program_id(0)]
            index = [tile_index(q_block, kp_ref[b], steps) for b in range(blocks)]
        for h in range(head_count):
            mine = (lane >= h * head_width) & (lane < (h + 1) * head_width)
            scores = dot_nt(jnp.where(mine, queries, jnp.zeros_like(queries)), k_ref[...]) + mask_row
            if with_bias:
                scores = scores + jnp.concatenate([b_ref[h, i] for i in index], axis=1)
            highest = jnp.max(scores, axis=-1, keepdims=True)
            powers = jnp.exp(scores - highest)
            total = jnp.sum(powers, axis=-1, keepdims=True)
            lse_ref[h] = highest + jnp.log(total)
            weights = (powers * (1.0 / total)).astype(bf16)
            result = jnp.where(mine, dot(weights, v_ref[...]), result)
        o_ref[...] = result.astype(bf16)

    whole = lambda *shape: pl.BlockSpec(shape, lambda i, *_: (0,) * len(shape))
    in_specs = [
        pl.BlockSpec((tile, width), lambda i, *_: (i, 0)),
        whole(keys, width),
        whole(keys, width),
        whole(1, keys),
    ]
    operands = [q, k, v, key_mask]
    if with_bias:
        in_specs.append(whole(*tiles.shape))
        operands.append(tiles)
    return pl.pallas_call(
        kernel,
        grid_spec=pltpu.PrefetchScalarGridSpec(
            num_scalar_prefetch=2 if with_bias else 0,
            grid=(rows // tile,),
            in_specs=in_specs,
            out_specs=[
                pl.BlockSpec((tile, width), lambda i, *_: (i, 0)),
                pl.BlockSpec((head_count, tile, 1), lambda i, *_: (0, i, 0)),
            ],
        ),
        out_shape=[
            jax.ShapeDtypeStruct((rows, width), bf16),
            jax.ShapeDtypeStruct((head_count, rows, 1), f32),
        ],
        name="attend",
    )(*(list(places) if with_bias else []), *operands)


def attend_back(q, k, v, key_mask, lse, grad_out, head_count, tile, places=None, tiles=None):
    rows, width = q.shape
    keys = k.shape[0]
    head_width = width // head_count
    with_bias = tiles is not None
    blocks = keys // tile if with_bias else 0
    steps = tiles.shape[1] - 1 if with_bias else 0
    grid = rows // tile

    def kernel(*refs):
        if with_bias:
            (qp_ref, kp_ref, q_ref, k_ref, v_ref, m_ref, lse_ref, g_ref, b_ref) = refs[:9]
            dq_ref, dk_ref, dv_ref, sums_ref, acc_ref = refs[9:]
        else:
            q_ref, k_ref, v_ref, m_ref, lse_ref, g_ref, dq_ref, dk_ref, dv_ref = refs
        step_id = pl.program_id(0)

        @pl.when(step_id == 0)
        def _():
            dk_ref[...] = jnp.zeros_like(dk_ref)
            dv_ref[...] = jnp.zeros_like(dv_ref)
            if with_bias:
                acc_ref[...] = jnp.zeros_like(acc_ref)

        lane = lax.broadcasted_iota(jnp.int32, (1, width), 1)
        queries = q_ref[...]
        grads = g_ref[...]
        mask_row = m_ref[...]
        result = jnp.zeros((tile, width), f32)
        if with_bias:
            q_block = qp_ref[step_id]
            index = [tile_index(q_block, kp_ref[b], steps) for b in range(blocks)]
        for h in range(head_count):
            mine = (lane >= h * head_width) & (lane < (h + 1) * head_width)
            q_head = jnp.where(mine, queries, jnp.zeros_like(queries))
            g_head = jnp.where(mine, grads, jnp.zeros_like(grads))
            scores = dot_nt(q_head, k_ref[...]) + mask_row
            if with_bias:
                scores = scores + jnp.concatenate([b_ref[h, i] for i in index], axis=1)
            prob = jnp.exp(scores - lse_ref[h])
            grad_prob = dot_nt(g_head, v_ref[...])
            row_dot = jnp.sum(prob * grad_prob, axis=-1, keepdims=True)
            grad_scores = prob * (grad_prob - row_dot)
            scores_b = grad_scores.astype(bf16)
            result = jnp.where(mine, dot(scores_b, k_ref[...]), result)
            dk_ref[...] += dot_tn(scores_b, q_head)
            dv_ref[...] += dot_tn(prob.astype(bf16), g_head)
            if with_bias:
                for b in range(blocks):
                    acc_ref[h, index[b]] += grad_scores[:, b * tile : (b + 1) * tile]
        dq_ref[...] = result.astype(bf16)

        if with_bias:

            @pl.when(step_id == grid - 1)
            def _():
                row = lax.broadcasted_iota(jnp.int32, (8, 2 * tile), 0)
                for h in range(head_count):
                    for s in range(steps):
                        x = jnp.concatenate(
                            [acc_ref[h, s], jnp.zeros((tile, tile), f32)], axis=1
                        )
                        n = tile
                        while n > 8:
                            n //= 2
                            x = x[:n] + pltpu.roll(x[n : 2 * n], 2 * tile - n, 1)
                        for bit in (4, 2, 1):
                            x = jnp.where((row & bit) != 0, pltpu.roll(x, 2 * tile - bit, 1), x)
                        sums_ref[h, s : s + 1, :] = jnp.sum(x, axis=0, keepdims=True)

    whole = lambda *shape: pl.BlockSpec(shape, lambda i, *_: (0,) * len(shape))
    part = pl.BlockSpec((tile, width), lambda i, *_: (i, 0))
    in_specs = [
        part,
        whole(keys, width),
        whole(keys, width),
        whole(1, keys),
        pl.BlockSpec((head_count, tile, 1), lambda i, *_: (0, i, 0)),
        part,
    ]
    operands = [q, k, v, key_mask, lse, grad_out]
    out_specs = [part, whole(keys, width), whole(keys, width)]
    out_shape = [
        jax.ShapeDtypeStruct((rows, width), bf16),
        jax.ShapeDtypeStruct((keys, width), f32),
        jax.ShapeDtypeStruct((keys, width), f32),
    ]
    scratch = []
    if with_bias:
        in_specs.append(whole(*tiles.shape))
        operands.append(tiles)
        out_specs.append(whole(head_count, steps, 2 * tile))
        out_shape.append(jax.ShapeDtypeStruct((head_count, steps, 2 * tile), f32))
        scratch.append(pltpu.VMEM((head_count, steps + 1, tile, tile), f32))
    return pl.pallas_call(
        kernel,
        grid_spec=pltpu.PrefetchScalarGridSpec(
            num_scalar_prefetch=2 if with_bias else 0,
            grid=(grid,),
            in_specs=in_specs,
            out_specs=out_specs,
            scratch_shapes=scratch,
        ),
        out_shape=out_shape,
        name="attend_back",
    )(*(list(places) if with_bias else []), *operands)


class Plane:
    def __init__(self, dp_size, ctx_size):
        self.size = dp_size * ctx_size
        ctx_bits = ctx_size.bit_length() - 1
        bits = self.size.bit_length() - 1
        low = list(range(ctx_bits))
        high = list(range(bits - 1, ctx_bits, -1))
        near = [ctx_bits] if bits > ctx_bits else []
        self.near = near
        self.orders = (low + high, high + low)
        self.me = lax.axis_index("dp") * ctx_size + lax.axis_index("ctx")

    def swap(self, x, bit):
        pairs = [(i, i ^ (1 << bit)) for i in range(self.size)]
        return lax.ppermute(x, ("dp", "ctx"), pairs)

    def gather(self, x):
        cols = x.shape[1]
        cut = max(128, cols // 2 // 128 * 128)
        halves = []
        for piece, order in zip((x[:, :cut], x[:, cut:]), self.orders):
            have, keys = piece[None], [0]
            for bit in order + self.near:
                got = self.swap(have, bit)
                have = jnp.concatenate([have, got], axis=0)
                keys = keys + [key ^ (1 << bit) for key in keys]
            where_is = {key: i for i, key in enumerate(keys)}
            table = jnp.array([where_is[key] for key in range(self.size)], jnp.int32)
            picked = [
                lax.dynamic_index_in_dim(have, table[b ^ self.me], 0, keepdims=False)
                for b in range(self.size)
            ]
            halves.append(picked)
        return cut, halves

    def gather_columns(self, x, widths):
        cut, halves = self.gather(x)
        results = []
        start = 0
        for width in widths:
            parts = []
            stop = start + width
            if start < cut:
                parts.append((0, start, min(stop, cut)))
            if stop > cut:
                parts.append((1, max(start, cut) - cut, stop - cut))
            rows = []
            for b in range(self.size):
                pieces = [halves[i][b][:, lo:hi] for i, lo, hi in parts]
                rows.append(pieces[0] if len(pieces) == 1 else jnp.concatenate(pieces, axis=1))
            results.append(jnp.concatenate(rows, axis=0))
            start = stop
        return results

    def scatter(self, grad):
        blocks = grad.reshape(self.size, -1, grad.shape[1])
        keys = list(range(self.size))
        take = lambda keep: jnp.stack(
            [lax.dynamic_index_in_dim(blocks, key ^ self.me, 0, keepdims=False) for key in keep]
        )
        if self.near:
            flag = 1 << self.near[0]
            kept = [key for key in keys if not key & flag]
            got = self.swap(take([key ^ flag for key in kept]), self.near[0])
            have, keys = take(kept).astype(f32) + got.astype(f32), kept
        else:
            have = take(keys).astype(f32)
        cols = grad.shape[1]
        cut = max(128, cols // 2 // 128 * 128)
        finals = []
        for span, order in zip((slice(0, cut), slice(cut, cols)), self.orders[::-1]):
            part, left = have[:, :, span], keys
            for bit in order:
                flag = 1 << bit
                stay = [i for i, key in enumerate(left) if not key & flag]
                leave = [left.index(left[i] ^ flag) for i in stay]
                pick = lambda ids: jnp.stack([part[i] for i in ids])
                got = self.swap(pick(leave).astype(bf16), bit)
                part = pick(stay) + got.astype(f32)
                left = [left[i] for i in stay]
            finals.append(part[0])
        return jnp.concatenate(finals, axis=1)

    def total(self, x):
        for bit in self.near + self.orders[0]:
            x = x + self.swap(x, bit)
        return x


def shards(
    inputs,
    encoded,
    seq_len,
    enc_len,
    norm_self,
    w_query,
    w_key,
    w_value,
    w_out,
    rel_table,
    norm_cross,
    c_query,
    c_key,
    c_value,
    c_out,
    norm_ff,
    w_gate,
    w_up,
    w_down,
    cotangent,
):
    seq_count, rows, width = inputs.shape
    assert seq_count == 1
    enc_rows = encoded.shape[1]
    bucket_count, heads = rel_table.shape
    tensor_size = lax.axis_size("tensor")
    ctx_size = lax.axis_size("ctx")
    shard_rows = w_query.shape[0]
    head_cols = w_query.shape[1]
    ff_cols = w_gate.shape[1]
    chunk = rows // tensor_size
    enc_chunk = enc_rows // tensor_size
    length = rows * ctx_size
    ti = lax.axis_index("tensor")
    ci = lax.axis_index("ctx")
    plane = Plane(lax.axis_size("dp"), ctx_size)
    others = list(range(1, tensor_size))

    def zswap(x, k):
        return lax.ppermute(x, "tensor", [(i, i ^ k) for i in range(tensor_size)])

    def cswap(x, c):
        return lax.ppermute(x, "ctx", [(i, i ^ c) for i in range(ctx_size)])

    def own_order(x):
        size = x.shape[0] // tensor_size
        return jnp.concatenate(
            [lax.dynamic_slice_in_dim(x, (ti ^ k) * size, size, 0) for k in range(tensor_size)], axis=0
        )

    def heads_to_tokens(x):
        size = x.shape[0] // tensor_size
        return jnp.concatenate(
            [x[:size]] + [zswap(x[k * size : (k + 1) * size], k) for k in others], axis=1
        )

    def tokens_to_heads(x):
        size = x.shape[1] // tensor_size
        return jnp.concatenate(
            [x[:, :size]] + [zswap(x[:, k * size : (k + 1) * size], k) for k in others], axis=0
        )

    def token_gather(x):
        return lax.optimization_barrier(
            jnp.concatenate([x] + [zswap(x, k) for k in others], axis=0)
        )

    def token_reduce(x):
        size = x.shape[0] // tensor_size
        total = x[:size]
        sent = x.astype(bf16)
        for k in others:
            total = total + zswap(sent[k * size : (k + 1) * size], k).astype(f32)
        return total

    def key_gather(x):
        return jnp.concatenate([x] + [cswap(x, c) for c in range(1, ctx_size)], axis=0)

    def key_reduce(x):
        size = x.shape[0] // ctx_size
        total = x[:size]
        for c in range(1, ctx_size):
            total = total + cswap(x[c * size : (c + 1) * size].astype(bf16), c).astype(f32)
        return total.astype(bf16)

    gains = jnp.stack([norm_self, norm_cross, norm_ff], axis=1)
    gains = jnp.pad(gains, ((0, 0), (0, 128 - 3)))
    first = jnp.concatenate([w_query, w_key, w_value, gains], axis=1)
    query_w, key_w, value_w, gain_cols = plane.gather_columns(first, [head_cols] * 3 + [128])
    gain_rows = gain_cols.astype(f32).T
    gain_one, gain_two, gain_three = (gain_rows[i : i + 1] for i in range(3))

    turned = jnp.concatenate([w_out.T, c_query, c_out.T], axis=1)
    turned_all = [turned] + [zswap(turned, k) for k in others]
    full = [
        jnp.concatenate([t[:, i * head_cols : (i + 1) * head_cols] for t in turned_all], axis=1)
        for i in range(3)
    ]
    second = jnp.concatenate([c_key, c_value] + full, axis=1)
    second, query_w = lax.optimization_barrier((second, query_w))
    ckey_w, cvalue_w, out_wt, cquery_w, cout_wt = plane.gather_columns(
        second, [head_cols] * 2 + [head_cols * tensor_size] * 3
    )
    third = jnp.concatenate([w_gate, w_up, w_down.T], axis=1)
    third, ckey_w = lax.optimization_barrier((third, ckey_w))
    gate_w, up_w, down_wt = plane.gather_columns(third, [ff_cols] * 3)

    blocks = jnp.arange(tensor_size, dtype=jnp.int32) ^ ti
    q_places = ci * tensor_size + blocks
    k_places = jnp.concatenate([(ci ^ c) * tensor_size + blocks for c in range(ctx_size)])
    within = jnp.arange(chunk, dtype=jnp.int32)
    row_positions = (q_places[:, None] * chunk + within[None, :]).reshape(-1)
    key_positions = (k_places[:, None] * chunk + within[None, :]).reshape(-1)
    enc_within = jnp.arange(enc_chunk, dtype=jnp.int32)
    enc_places = jnp.concatenate([(ci ^ c) * tensor_size + blocks for c in range(ctx_size)])
    enc_positions = (enc_places[:, None] * enc_chunk + enc_within[None, :]).reshape(-1)
    live = (row_positions < seq_len[0]).astype(f32)[:, None]
    self_mask = jnp.where(key_positions < seq_len[0], 0.0, MASKED).astype(f32)[None]
    cross_mask = jnp.where(enc_positions < enc_len[0], 0.0, MASKED).astype(f32)[None]

    steps = length // chunk
    lag = jnp.arange(2 * chunk, dtype=jnp.int32)
    lag = jnp.where(lag < chunk, -lag, 2 * chunk - lag)
    distance = jnp.maximum(jnp.arange(steps, dtype=jnp.int32)[:, None] * chunk + lag[None, :], 0)
    lag_bucket = bucket_of(distance)
    vectors = jnp.zeros((heads,) + distance.shape, f32)
    for bucket in range(bucket_count):
        vectors = jnp.where(lag_bucket[None] == bucket, rel_table[bucket][:, None, None], vectors)
    tiles = bias_tiles(vectors, chunk)
    places = (q_places, k_places)

    hidden_in = own_order(inputs[0]).astype(f32)
    enc = own_order(encoded[0])
    normed_one, rescale_one, input_one = rms_norm(hidden_in, gain_one)
    query_one = dot(input_one, query_w).astype(bf16)
    key_all = key_gather(dot(input_one, key_w).astype(bf16))
    value_all = key_gather(dot(input_one, value_w).astype(bf16))
    ckey_all = key_gather(dot(enc, ckey_w).astype(bf16))
    cvalue_all = key_gather(dot(enc, cvalue_w).astype(bf16))
    attn_one, total_one = attend(
        query_one, key_all, value_all, self_mask, heads, chunk, places, tiles
    )
    flat_one = heads_to_tokens(attn_one)
    hidden_one = hidden_in[:chunk] + dot_nt(flat_one, out_wt)
    normed_two, rescale_two, input_two = rms_norm(hidden_one, gain_two)
    query_two = tokens_to_heads(dot(input_two, cquery_w).astype(bf16))
    attn_two, total_two = attend(query_two, ckey_all, cvalue_all, cross_mask, heads, chunk)
    flat_two = heads_to_tokens(attn_two)
    hidden_two = hidden_one + dot_nt(flat_two, cout_wt)
    normed_three, rescale_three, input_three = rms_norm(hidden_two, gain_three)
    input_three = token_gather(input_three)
    gate_pre = dot(input_three, gate_w)
    up_pre = dot(input_three, up_w)
    gelu_value, gelu_slope = gelu_parts(gate_pre)
    ff_hidden = (gelu_value * up_pre).astype(bf16)
    ff_term = dot_nt(ff_hidden, down_wt)

    grad_out = own_order(cotangent[0]).astype(f32) * live
    grad_out_b = grad_out.astype(bf16)
    grad_ff = dot(grad_out_b, down_wt)
    grad_gate = (grad_ff * up_pre * gelu_slope).astype(bf16)
    grad_up = (grad_ff * gelu_value).astype(bf16)
    grad_normed_three = token_reduce(dot_nt(grad_gate, gate_w) + dot_nt(grad_up, up_w))
    layer_rows = (hidden_two + token_reduce(ff_term)).astype(bf16)
    layer_out = own_order(token_gather(layer_rows))
    grad_ff_w = jnp.concatenate(
        [
            dot_tn(input_three, grad_gate).astype(bf16),
            dot_tn(input_three, grad_up).astype(bf16),
            dot_tn(grad_out_b, ff_hidden).astype(bf16),
        ],
        axis=1,
    )
    ff_sum = plane.scatter(grad_ff_w)

    grad_gain_three = jnp.sum(grad_normed_three * normed_three, axis=0)
    back_three = norm_back(grad_normed_three, normed_three, rescale_three, gain_three)
    grad_two = grad_out[:chunk] + back_three
    grad_two_b = grad_two.astype(bf16)
    grad_cout = dot_tn(grad_two_b, flat_two).astype(bf16)
    grad_attn_two = tokens_to_heads(dot(grad_two_b, cout_wt).astype(bf16))
    query_grad_two, key_grad_two, value_grad_two = attend_back(
        query_two, ckey_all, cvalue_all, cross_mask, total_two, grad_attn_two, heads, chunk
    )
    query_grad_two = heads_to_tokens(query_grad_two)
    grad_normed_two = dot_nt(query_grad_two, cquery_w)
    grad_gain_two = jnp.sum(grad_normed_two * normed_two, axis=0)
    back_two = norm_back(grad_normed_two, normed_two, rescale_two, gain_two)
    grad_one = grad_two + back_two
    grad_one_b = grad_one.astype(bf16)
    grad_attn_one = tokens_to_heads(dot(grad_one_b, out_wt).astype(bf16))

    key_grad_two = key_reduce(key_grad_two)
    value_grad_two = key_reduce(value_grad_two)
    grad_cquery = dot_tn(input_two, query_grad_two).astype(bf16)
    grad_ckey = dot_tn(enc, key_grad_two).astype(bf16)
    grad_cvalue = dot_tn(enc, value_grad_two).astype(bf16)
    cross_sum = plane.scatter(
        jnp.concatenate([grad_ckey, grad_cvalue, grad_cout, grad_cquery], axis=1)
    )
    enc_partial = dot_nt(key_grad_two, ckey_w) + dot_nt(value_grad_two, cvalue_w)
    grad_encoded = own_order(token_gather(token_reduce(enc_partial).astype(bf16))).astype(f32)

    query_grad_one, key_grad_one, value_grad_one, lag_sums = attend_back(
        query_one,
        key_all,
        value_all,
        self_mask,
        total_one,
        grad_attn_one,
        heads,
        chunk,
        places,
        tiles,
    )
    out_sum = plane.scatter(dot_tn(grad_one_b, flat_one).astype(bf16))
    key_grad_one = key_reduce(key_grad_one)
    value_grad_one = key_reduce(value_grad_one)
    dn_partial = (
        dot_nt(query_grad_one, query_w)
        + dot_nt(key_grad_one, key_w)
        + dot_nt(value_grad_one, value_w)
    )
    grad_normed_one = token_reduce(dn_partial)
    grad_gain_one = jnp.sum(grad_normed_one * normed_one[:chunk], axis=0)
    back_one = norm_back(grad_normed_one, normed_one[:chunk], rescale_one[:chunk], gain_one)
    grad_rows = (grad_one + back_one).astype(bf16)
    grad_inputs = own_order(token_gather(grad_rows)).astype(f32)
    self_sum = plane.scatter(
        jnp.concatenate(
            [
                dot_tn(input_one, query_grad_one).astype(bf16),
                dot_tn(input_one, key_grad_one).astype(bf16),
                dot_tn(input_one, value_grad_one).astype(bf16),
            ],
            axis=1,
        )
    )

    selector = (
        lag_bucket.reshape(-1)[:, None] == jnp.arange(bucket_count, dtype=jnp.int32)[None, :]
    ).astype(f32)
    table_term = lax.dot_general(
        selector,
        lag_sums.reshape(heads, -1),
        (((0,), (1,)), ((), ())),
        precision=lax.Precision.HIGHEST,
        preferred_element_type=f32,
    )
    grad_rel_table = plane.total(table_term)
    small = plane.total(jnp.stack([grad_gain_one, grad_gain_two, grad_gain_three]))
    bit = 1
    while bit < tensor_size:
        small = small + zswap(small, bit)
        bit *= 2
    small = lax.dynamic_slice_in_dim(small, plane.me * shard_rows, shard_rows, 1)

    def head_block_sum(full_grad):
        parts = full_grad.reshape(shard_rows, -1, tensor_size, head_cols)
        total = parts[:, :, 0]
        for k in others:
            total = total + zswap(parts[:, :, k].astype(bf16), k).astype(f32)
        return total

    cross_full = head_block_sum(cross_sum[:, 2 * head_cols :])
    out_full = head_block_sum(out_sum)
    cut = lambda x, i, w: x[:, i * w : (i + 1) * w]
    return (
        layer_out[None],
        grad_inputs[None],
        grad_encoded[None],
        small[0],
        cut(self_sum, 0, head_cols),
        cut(self_sum, 1, head_cols),
        cut(self_sum, 2, head_cols),
        out_full[:, 0].T,
        grad_rel_table,
        small[1],
        cross_full[:, 1],
        cut(cross_sum, 0, head_cols),
        cut(cross_sum, 1, head_cols),
        cross_full[:, 0].T,
        small[2],
        cut(ff_sum, 0, ff_cols),
        cut(ff_sum, 1, ff_cols),
        cut(ff_sum, 2, ff_cols).T,
    )


def solution(mesh):
    rows_in = P(("dp", "ctx"), "tensor")
    rows_out = P("tensor", ("dp", "ctx"))
    gain = P(("dp", "ctx"))
    token = P("dp", "ctx", None)
    table = P(None, "tensor")
    return jax.shard_map(
        shards,
        mesh=mesh,
        in_specs=(
            token,
            token,
            P("dp"),
            P("dp"),
            gain,
            rows_in,
            rows_in,
            rows_in,
            rows_out,
            table,
            gain,
            rows_in,
            rows_in,
            rows_in,
            rows_out,
            gain,
            rows_in,
            rows_in,
            rows_out,
            token,
        ),
        out_specs=(
            token,
            token,
            token,
            gain,
            rows_in,
            rows_in,
            rows_in,
            rows_out,
            table,
            gain,
            rows_in,
            rows_in,
            rows_in,
            rows_out,
            gain,
            rows_in,
            rows_in,
            rows_out,
        ),
        check_vma=False,
    )
```

```python
import math

import numpy as np

import jax
import jax.numpy as jnp
from jax import lax
from jax.experimental import pallas as pl
from jax.experimental.pallas import tpu as pltpu
from jax.sharding import PartitionSpec as P

bf16 = jnp.bfloat16
f32 = jnp.float32
MASKED = -1e30


bucket_edges = list(range(1, 17)) + [
    math.ceil(16.0 * 8.0 ** ((bucket_index - 16) / 16.0)) for bucket_index in range(17, 32)
]


def lag_buckets(steps, tile):
    lag = np.arange(2 * tile)
    lag = np.where(lag < tile, -lag, 2 * tile - lag)
    distance = np.maximum(np.arange(steps)[:, None] * tile + lag[None, :], 0)
    return np.searchsorted(np.array(bucket_edges), distance, side="right")


def dot(a, b):
    return lax.dot_general(a, b, (((1,), (0,)), ((), ())), preferred_element_type=f32)


def dot_nt(a, b):
    return lax.dot_general(a, b, (((1,), (1,)), ((), ())), preferred_element_type=f32)


def dot_tn(a, b):
    return lax.dot_general(a, b, (((0,), (0,)), ((), ())), preferred_element_type=f32)


def rms_norm(hidden, gain):
    rescale = lax.rsqrt(jnp.mean(hidden * hidden, axis=-1, keepdims=True) + 1e-06)
    normed = hidden * rescale
    return normed, rescale, (normed * gain).astype(bf16)


def gelu_parts(preact):
    argument = 0.7978845608028654 * (preact + 0.044715 * preact * preact * preact)
    tangent = jnp.tanh(argument)
    gelu_value = 0.5 * preact * (1.0 + tangent)
    gelu_slope = 0.5 * (1.0 + tangent) + 0.5 * preact * (
        1.0 - tangent * tangent
    ) * 0.7978845608028654 * (1.0 + 3.0 * 0.044715 * preact * preact)
    return gelu_value, gelu_slope


def bias_tiles(vectors, tile):
    heads, steps, width = vectors.shape

    def kernel(v_ref, out_ref):
        row = lax.broadcasted_iota(jnp.int32, (tile, tile), 0)
        col = lax.broadcasted_iota(jnp.int32, (tile, tile), 1)
        for step in range(steps):
            spread = jnp.broadcast_to(v_ref[0, step : step + 1, :], (tile, width))
            skewed = pltpu.roll(spread, 0, 1, stride=1, stride_axis=0)[:, :tile]
            if step == 0:
                skewed = jnp.where(col <= row, skewed, MASKED)
            out_ref[0, step] = skewed
        out_ref[0, steps] = jnp.full((tile, tile), MASKED, f32)

    return pl.pallas_call(
        kernel,
        grid=(heads,),
        in_specs=[pl.BlockSpec((1, steps, width), lambda h: (h, 0, 0))],
        out_specs=pl.BlockSpec((1, steps + 1, tile, tile), lambda h: (h, 0, 0, 0)),
        out_shape=jax.ShapeDtypeStruct((heads, steps + 1, tile, tile), f32),
        name="bias_tiles",
    )(vectors)


def tile_index(q_block, k_block, steps):
    delta = q_block - k_block
    return jnp.where(delta >= 0, delta, steps)


def whole_spec(x):
    shape = x.shape
    return pl.BlockSpec(shape, lambda *_: (0,) * len(shape))


def attend(q_parts, kv_parts, key_mask, head_count, parts, places=None, tiles=None):
    width = q_parts[0].shape[1]
    rows = sum(x.shape[0] for x in q_parts)
    keys = sum(x.shape[0] for x in kv_parts)
    tile = rows // parts
    head_width = width // head_count
    with_bias = tiles is not None
    blocks = keys // tile if with_bias else 0
    steps = tiles.shape[1] - 1 if with_bias else 0
    nq, nkv = len(q_parts), len(kv_parts)

    def kernel(*refs):
        refs = list(refs)
        if with_bias:
            qp_ref, kp_ref = refs[:2]
            refs = refs[2:]
        q_refs, kv_refs, refs = refs[:nq], refs[nq : nq + nkv], refs[nq + nkv :]
        m_ref = refs.pop(0)
        b_ref = refs.pop(0) if with_bias else None
        o_refs, lse_ref = refs[:parts], refs[parts]
        q_s, k_s, v_s, o_s = refs[parts + 1 :]
        gather_rows(q_refs, q_s)
        split_rows(kv_refs, k_s, v_s)
        lane = lax.broadcasted_iota(jnp.int32, (1, width), 1)
        mask_row = m_ref[...]

        def body(i, carry):
            here = pl.ds(pl.multiple_of(i * tile, tile), tile)
            queries = q_s[here, :]
            result = jnp.zeros((tile, width), f32)
            if with_bias:
                index = [tile_index(qp_ref[i], kp_ref[b], steps) for b in range(blocks)]
            for h in range(head_count):
                mine = (lane >= h * head_width) & (lane < (h + 1) * head_width)
                scores = dot_nt(jnp.where(mine, queries, jnp.zeros_like(queries)), k_s[...]) + mask_row
                if with_bias:
                    scores = scores + jnp.concatenate([b_ref[h, b] for b in index], axis=1)
                highest = jnp.max(scores, axis=-1, keepdims=True)
                powers = jnp.exp(scores - highest)
                total = jnp.sum(powers, axis=-1, keepdims=True)
                lse_ref[h, here, :] = highest + jnp.log(total)
                weights = (powers * (1.0 / total)).astype(bf16)
                result = jnp.where(mine, dot(weights, v_s[...]), result)
            o_s[here, :] = result.astype(bf16)
            return carry

        lax.fori_loop(0, parts, body, 0)
        for p in range(parts):
            o_refs[p][...] = o_s[p * tile : (p + 1) * tile, :]

    operands = list(q_parts) + list(kv_parts) + [key_mask] + ([tiles] if with_bias else [])
    part = jax.ShapeDtypeStruct((tile, width), bf16)
    lse = jax.ShapeDtypeStruct((head_count, rows, 1), f32)
    out_shape = [part] * parts + [lse]
    results = pl.pallas_call(
        kernel,
        grid_spec=pltpu.PrefetchScalarGridSpec(
            num_scalar_prefetch=2 if with_bias else 0,
            grid=(1,),
            in_specs=[whole_spec(x) for x in operands],
            out_specs=[whole_spec(x) for x in out_shape],
            scratch_shapes=[
                pltpu.VMEM((rows, width), bf16),
                pltpu.VMEM((keys, width), bf16),
                pltpu.VMEM((keys, width), bf16),
                pltpu.VMEM((rows, width), bf16),
            ],
        ),
        out_shape=out_shape,
        name="attend",
    )(*(list(places) if with_bias else []), *operands)
    return results[:parts], results[parts]


def gather_rows(refs, target):
    at = 0
    for ref in refs:
        target[at : at + ref.shape[0], :] = ref[...]
        at += ref.shape[0]


def split_rows(refs, left, right):
    at = 0
    width = left.shape[1]
    for ref in refs:
        both = ref[...]
        left[at : at + ref.shape[0], :] = both[:, :width]
        right[at : at + ref.shape[0], :] = both[:, width:]
        at += ref.shape[0]


def attend_back(q_parts, kv_parts, key_mask, lse, g_parts, head_count, split, places=None, tiles=None):
    width = q_parts[0].shape[1]
    rows = sum(x.shape[0] for x in q_parts)
    keys = sum(x.shape[0] for x in kv_parts)
    parts = len(g_parts)
    tile = rows // parts
    own_keys = kv_parts[0].shape[0]
    head_width = width // head_count
    with_bias = tiles is not None
    blocks = keys // tile if with_bias else 0
    steps = tiles.shape[1] - 1 if with_bias else 0
    nq, nkv = len(q_parts), len(kv_parts)
    outs_q = parts if split else 1

    def kernel(*refs):
        refs = list(refs)
        take = lambda n: [refs.pop(0) for _ in range(n)]
        if with_bias:
            qp_ref, kp_ref = take(2)
        q_refs, kv_refs, g_refs = take(nq), take(nkv), take(parts)
        m_ref, lse_ref = take(2)
        b_ref = refs.pop(0) if with_bias else None
        dq_refs = take(outs_q)
        own_ref = refs.pop(0)
        sent_refs = take(nkv - 1)
        sums_ref = refs.pop(0) if with_bias else None
        q_s, k_s, v_s, g_s, dq_s, dk_s, dv_s = take(7)
        acc_ref = refs.pop(0) if with_bias else None
        gather_rows(q_refs, q_s)
        gather_rows(g_refs, g_s)
        split_rows(kv_refs, k_s, v_s)
        dk_s[...] = jnp.zeros_like(dk_s)
        dv_s[...] = jnp.zeros_like(dv_s)
        if with_bias:
            acc_ref[...] = jnp.zeros_like(acc_ref)
        lane = lax.broadcasted_iota(jnp.int32, (1, width), 1)
        mask_row = m_ref[...]

        def body(i, carry):
            here = pl.ds(pl.multiple_of(i * tile, tile), tile)
            queries = q_s[here, :]
            grads = g_s[here, :]
            result = jnp.zeros((tile, width), f32)
            if with_bias:
                index = [tile_index(qp_ref[i], kp_ref[b], steps) for b in range(blocks)]
            for h in range(head_count):
                mine = (lane >= h * head_width) & (lane < (h + 1) * head_width)
                q_head = jnp.where(mine, queries, jnp.zeros_like(queries))
                g_head = jnp.where(mine, grads, jnp.zeros_like(grads))
                scores = dot_nt(q_head, k_s[...]) + mask_row
                if with_bias:
                    scores = scores + jnp.concatenate([b_ref[h, b] for b in index], axis=1)
                prob = jnp.exp(scores - lse_ref[h, here, :])
                grad_prob = dot_nt(g_head, v_s[...])
                row_dot = jnp.sum(prob * grad_prob, axis=-1, keepdims=True)
                grad_scores = prob * (grad_prob - row_dot)
                scores_b = grad_scores.astype(bf16)
                result = jnp.where(mine, dot(scores_b, k_s[...]), result)
                dk_s[...] += dot_tn(scores_b, q_head)
                dv_s[...] += dot_tn(prob.astype(bf16), g_head)
                if with_bias:
                    for b in range(blocks):
                        acc_ref[h, index[b]] += grad_scores[:, b * tile : (b + 1) * tile]
            dq_s[here, :] = result.astype(bf16)
            return carry

        lax.fori_loop(0, parts, body, 0)
        for p in range(outs_q):
            size = rows // outs_q
            dq_refs[p][...] = dq_s[p * size : (p + 1) * size, :]
        own_ref[:, :width] = dk_s[:own_keys, :]
        own_ref[:, width:] = dv_s[:own_keys, :]
        for c in range(1, nkv):
            sent_refs[c - 1][:, :width] = dk_s[c * own_keys : (c + 1) * own_keys, :].astype(bf16)
            sent_refs[c - 1][:, width:] = dv_s[c * own_keys : (c + 1) * own_keys, :].astype(bf16)
        if with_bias:
            row = lax.broadcasted_iota(jnp.int32, (8, 2 * tile), 0)
            for h in range(head_count):
                for s in range(steps):
                    x = jnp.concatenate([acc_ref[h, s], jnp.zeros((tile, tile), f32)], axis=1)
                    n = tile
                    while n > 8:
                        n //= 2
                        x = x[:n] + pltpu.roll(x[n : 2 * n], 2 * tile - n, 1)
                    for bit in (4, 2, 1):
                        x = jnp.where((row & bit) != 0, pltpu.roll(x, 2 * tile - bit, 1), x)
                    sums_ref[h, s : s + 1, :] = jnp.sum(x, axis=0, keepdims=True)

    operands = list(q_parts) + list(kv_parts) + list(g_parts) + [key_mask, lse]
    out_shape = [jax.ShapeDtypeStruct((rows // outs_q, width), bf16)] * outs_q
    out_shape.append(jax.ShapeDtypeStruct((own_keys, 2 * width), f32))
    out_shape += [jax.ShapeDtypeStruct((own_keys, 2 * width), bf16)] * (nkv - 1)
    scratch = [pltpu.VMEM((rows, width), bf16)]
    scratch += [pltpu.VMEM((keys, width), bf16)] * 2
    scratch += [pltpu.VMEM((rows, width), bf16)] * 2
    scratch += [pltpu.VMEM((keys, width), f32)] * 2
    if with_bias:
        operands.append(tiles)
        out_shape.append(jax.ShapeDtypeStruct((head_count, steps, 2 * tile), f32))
        scratch.append(pltpu.VMEM((head_count, steps + 1, tile, tile), f32))
    results = pl.pallas_call(
        kernel,
        grid_spec=pltpu.PrefetchScalarGridSpec(
            num_scalar_prefetch=2 if with_bias else 0,
            grid=(1,),
            in_specs=[whole_spec(x) for x in operands],
            out_specs=[whole_spec(x) for x in out_shape],
            scratch_shapes=scratch,
        ),
        out_shape=out_shape,
        name="attend_back",
    )(*(list(places) if with_bias else []), *operands)
    dq, results = results[:outs_q], results[outs_q:]
    own, sent, rest = results[0], results[1:nkv], results[nkv:]
    return dq, own, sent, (rest[0] if with_bias else None)


def lay_columns(refs, target):
    at = 0
    for ref in refs:
        target[:, at : at + ref.shape[1]] = ref[...]
        at += ref.shape[1]


def stage_out(blocks, weight_t, residual, gain, next_w):
    count = len(blocks)
    rows, cols = blocks[0].shape
    width = residual.shape[1]
    more = next_w is not None

    def kernel(*refs):
        refs = list(refs)
        b_refs = [refs.pop(0) for _ in range(count)]
        w_ref, res_ref, g_ref = [refs.pop(0) for _ in range(3)]
        n_ref = refs.pop(0) if more else None
        flat_ref, hid_ref, inp_ref = refs[:3]
        lay_columns(b_refs, flat_ref)
        hidden = res_ref[...] + dot_nt(flat_ref[...], w_ref[...])
        hid_ref[...] = hidden
        normed, rescale, scaled = rms_norm(hidden, g_ref[...])
        inp_ref[...] = scaled
        if more:
            following = dot(scaled, n_ref[...]).astype(bf16)
            for k in range(count):
                refs[3 + k][...] = following[:, k * cols : (k + 1) * cols]

    operands = list(blocks) + [weight_t, residual, gain] + ([next_w] if more else [])
    specs = [whole_spec(x) for x in operands]
    specs[count + 1] = pl.BlockSpec((rows, width), lambda *_: (0, 0))
    out_shape = [
        jax.ShapeDtypeStruct((rows, count * cols), bf16),
        jax.ShapeDtypeStruct((rows, width), f32),
        jax.ShapeDtypeStruct((rows, width), bf16),
    ] + ([jax.ShapeDtypeStruct((rows, cols), bf16)] * count if more else [])
    results = pl.pallas_call(
        kernel,
        grid=(1,),
        in_specs=specs,
        out_specs=[whole_spec(x) for x in out_shape],
        out_shape=out_shape,
        name="stage_out",
    )(*operands)
    return results[0], results[1], results[2], results[3:]


def stage_back(own, others, weight, hidden, gain, upstream, next_wt, count, with_gain):
    rows = others[0].shape[0]
    width = hidden.shape[1]
    nb = 1 + len(others)
    more = next_wt is not None
    cols = next_wt.shape[1] // count if more else 0

    def kernel(*refs):
        refs = list(refs)
        take = lambda n: [refs.pop(0) for _ in range(n)]
        in_refs = take(nb)
        w_ref = refs.pop(0) if weight is not None else None
        h_ref, g_ref, u_ref = take(3)
        n_ref = refs.pop(0) if more else None
        grad_ref = refs.pop(0)
        if weight is not None:
            flat_ref = refs.pop(0)
            lay_columns(in_refs, flat_ref)
            dn = dot_nt(flat_ref[...], w_ref[...])
        else:
            dn = in_refs[0][...]
            for ref in in_refs[1:]:
                dn = dn + ref[...].astype(f32)
        h = h_ref[...].astype(f32)
        rescale = lax.rsqrt(jnp.mean(h * h, axis=-1, keepdims=True) + 1e-06)
        normed = h * rescale
        scaled = dn * g_ref[...]
        back = rescale * (scaled - normed * jnp.mean(scaled * normed, axis=-1, keepdims=True))
        grad = u_ref[...] + back
        if with_gain:
            refs.pop(0)[...] = jnp.sum(dn * normed, axis=0, keepdims=True)
        if more:
            grad_ref[...] = grad
            rounded = grad.astype(bf16)
            refs.pop(0)[...] = rounded
            following = dot(rounded, n_ref[...]).astype(bf16)
            for k in range(count):
                refs[k][...] = following[:, k * cols : (k + 1) * cols]
        else:
            grad_ref[...] = grad.astype(bf16)

    operands = [own] + list(others) + ([weight] if weight is not None else [])
    at = len(operands)
    operands += [hidden, gain, upstream] + ([next_wt] if more else [])
    specs = [whole_spec(x) for x in operands]
    chunk_spec = pl.BlockSpec((rows, width), lambda *_: (0, 0))
    specs[at] = chunk_spec
    specs[at + 2] = chunk_spec
    if weight is None:
        specs[0] = chunk_spec
    out_shape = [jax.ShapeDtypeStruct((rows, width), f32 if more else bf16)]
    if weight is not None:
        out_shape.append(jax.ShapeDtypeStruct((rows, weight.shape[1]), bf16))
    if with_gain:
        out_shape.append(jax.ShapeDtypeStruct((1, width), f32))
    if more:
        out_shape.append(jax.ShapeDtypeStruct((rows, width), bf16))
        out_shape += [jax.ShapeDtypeStruct((rows, cols), bf16)] * count
    return pl.pallas_call(
        kernel,
        grid=(1,),
        in_specs=specs,
        out_specs=[whole_spec(x) for x in out_shape],
        out_shape=out_shape,
        name="stage_back",
    )(*operands)


def tie(first, second):
    return lax.optimization_barrier((first, second))


class Plane:
    def __init__(self, dp_size, ctx_size):
        self.size = dp_size * ctx_size
        ctx_bits = ctx_size.bit_length() - 1
        bits = self.size.bit_length() - 1
        low = list(range(ctx_bits))
        high = list(range(bits - 1, ctx_bits, -1))
        self.near = ctx_bits if bits > ctx_bits else bits - 1
        if bits == ctx_bits:
            low = low[:-1]
        self.orders = (low + high, high + low)
        self.me = lax.axis_index("dp") * ctx_size + lax.axis_index("ctx")
        flag = 1 << self.near
        self.kept = [key for key in range(self.size) if not key & flag]

    def swap(self, x, bit):
        pairs = [(i, i ^ (1 << bit)) for i in range(self.size)]
        return lax.ppermute(x, ("dp", "ctx"), pairs)

    def cut(self, cols):
        return max(128, cols // 2 // 128 * 128)

    def gather_start(self, x):
        cut = self.cut(x.shape[1])
        return [[x[:, :cut][None], [0], None], [x[:, cut:][None], [0], None]]

    def gather_step(self, state, step):
        for half, order in zip(state, self.orders):
            bit = order[step] if step < len(order) else self.near
            half[2] = self.swap(half[0], bit)
        return state

    def gather_join(self, state, step):
        for half, order in zip(state, self.orders):
            half[0] = jnp.concatenate([half[0], half[2]], axis=0)
            half[1] = half[1] + [key ^ (1 << order[step]) for key in half[1]]
        return state

    def assemble(self, state, widths):
        rows = state[0][0].shape[1]
        size, near = self.size, self.near
        cut = state[0][0].shape[2]
        orders = self.orders
        if rows % 16:
            return self.assemble_plain(state, widths)

        def kernel(me_ref, *refs):
            halves = (refs[0:2], refs[2:4])
            outs = refs[4:]
            for b in range(size):
                key = me_ref[0] ^ b
                values = []
                for (old, new), order in zip(halves, orders):
                    place = jnp.int32(0)
                    for j, bit in enumerate(order):
                        place = place | (((key >> bit) & 1) << j)
                    newer = ((key >> near) & 1) == 1
                    values.append(jnp.where(newer, new[place], old[place]))
                start = 0
                for out, width in zip(outs, widths):
                    stop = start + width
                    lo, hi = min(start, cut), min(stop, cut)
                    if hi > lo:
                        out[b * rows : (b + 1) * rows, : hi - lo] = values[0][:, lo:hi]
                    if stop > cut:
                        from_ = max(start, cut)
                        out[b * rows : (b + 1) * rows, from_ - start :] = values[1][:, from_ - cut : stop - cut]
                    start = stop

        operands = [state[0][0], state[0][2], state[1][0], state[1][2]]
        out_shape = [jax.ShapeDtypeStruct((size * rows, w), bf16) for w in widths]
        return pl.pallas_call(
            kernel,
            grid_spec=pltpu.PrefetchScalarGridSpec(
                num_scalar_prefetch=1,
                grid=(1,),
                in_specs=[whole_spec(x) for x in operands],
                out_specs=[whole_spec(x) for x in out_shape],
            ),
            out_shape=out_shape,
            name="assemble",
        )(self.me[None], *operands)

    def assemble_plain(self, state, widths):
        halves = []
        for half, order in zip(state, self.orders):
            have = jnp.concatenate([half[0], half[2]], axis=0)
            rows = []
            for b in range(self.size):
                key = self.me ^ b
                place = jnp.int32(0)
                for j, bit in enumerate(order + [self.near]):
                    place = place | (((key >> bit) & 1) << j)
                rows.append(lax.dynamic_index_in_dim(have, place, 0, keepdims=False))
            halves.append(jnp.concatenate(rows, axis=0))
        both = jnp.concatenate(halves, axis=1)
        starts = np.cumsum([0] + list(widths))
        return [both[:, lo : lo + w] for lo, w in zip(starts, widths)]

    def pack(self, pairs, rows):
        widths = [g.shape[1] for _, g in pairs]
        total = sum(widths)
        features = pairs[0][0].shape[1]
        kept = self.kept
        flag = 1 << self.near
        if rows % 16:
            grad = jnp.concatenate([dot_tn(x, g).astype(bf16) for x, g in pairs], axis=1)
            grad = grad.reshape(self.size, rows, total)
            take = lambda bit: jnp.stack(
                [lax.dynamic_index_in_dim(grad, self.me ^ key ^ bit, 0, keepdims=False) for key in kept]
            )
            return take(0), take(flag)

        def kernel(me_ref, *refs):
            keep_ref, send_ref, acc_ref = refs[2 * len(pairs) :]
            start = 0
            for i, width in enumerate(widths):
                acc_ref[:, start : start + width] = dot_tn(refs[2 * i][...], refs[2 * i + 1][...])
                start += width
            for place, key in enumerate(kept):
                mine = me_ref[0] ^ key
                keep_ref[place] = acc_ref[pl.ds(mine * rows, rows), :].astype(bf16)
                send_ref[place] = acc_ref[pl.ds((mine ^ flag) * rows, rows), :].astype(bf16)

        operands = [x for pair in pairs for x in pair]
        out = jax.ShapeDtypeStruct((len(kept), rows, total), bf16)
        return pl.pallas_call(
            kernel,
            grid_spec=pltpu.PrefetchScalarGridSpec(
                num_scalar_prefetch=1,
                grid=(1,),
                in_specs=[whole_spec(x) for x in operands],
                out_specs=[whole_spec(out)] * 2,
                scratch_shapes=[pltpu.VMEM((features, total), f32)],
            ),
            out_shape=[out, out],
            name="pack",
        )(self.me[None], *operands)


class Scatter:
    def __init__(self, plane, packed):
        self.plane = plane
        keep, send = packed
        self.state = [[keep, plane.kept, None, send]]
        self.orders = [[plane.near]]
        self.split = False

    def launch(self):
        for half, order in zip(self.state, self.orders):
            half[2] = self.plane.swap(half[3], order[0])
        return self

    @property
    def pending(self):
        return [half[2] for half in self.state]

    @pending.setter
    def pending(self, values):
        for half, value in zip(self.state, values):
            half[2] = value

    @property
    def outgoing(self):
        return [half[3] for half in self.state]

    @outgoing.setter
    def outgoing(self, values):
        for half, value in zip(self.state, values):
            half[3] = value

    def absorb(self):
        for half in self.state:
            half[0] = half[0].astype(f32) + half[2].astype(f32)
        if not self.split:
            have, keys = self.state[0][0], self.state[0][1]
            cut = self.plane.cut(have.shape[2])
            self.state = [[have[:, :, :cut], keys, None, None], [have[:, :, cut:], keys, None, None]]
            self.orders = [list(order) for order in self.plane.orders[::-1]]
            self.split = True
        else:
            self.orders = [order[1:] for order in self.orders]
        for half, order in zip(self.state, self.orders):
            if not order:
                continue
            part, keys = half[0], half[1]
            flag = 1 << order[0]
            stay = [i for i, key in enumerate(keys) if not key & flag]
            leave = [keys.index(keys[i] ^ flag) for i in stay]
            pick = lambda ids: jnp.concatenate([part[i : i + 1] for i in ids], axis=0)
            half[3] = pick(leave).astype(bf16)
            half[0] = pick(stay)
            half[1] = [keys[i] for i in stay]
        return self

    @property
    def open(self):
        return not self.split or bool(self.orders[0])

    def finish(self):
        while self.open:
            self.launch()
            self.absorb()
        return jnp.concatenate([half[0][0] for half in self.state], axis=1)


def shards(
    inputs,
    encoded,
    seq_len,
    enc_len,
    norm_self,
    w_query,
    w_key,
    w_value,
    w_out,
    rel_table,
    norm_cross,
    c_query,
    c_key,
    c_value,
    c_out,
    norm_ff,
    w_gate,
    w_up,
    w_down,
    cotangent,
):
    seq_count, rows, width = inputs.shape
    assert seq_count == 1
    enc_rows = encoded.shape[1]
    bucket_count, heads = rel_table.shape
    tensor_size = lax.axis_size("tensor")
    ctx_size = lax.axis_size("ctx")
    shard_rows = w_query.shape[0]
    head_cols = w_query.shape[1]
    ff_cols = w_gate.shape[1]
    all_heads = head_cols * tensor_size
    chunk = rows // tensor_size
    enc_chunk = enc_rows // tensor_size
    length = rows * ctx_size
    ti = lax.axis_index("tensor")
    ci = lax.axis_index("ctx")
    plane = Plane(lax.axis_size("dp"), ctx_size)
    others = list(range(1, tensor_size))
    order_index = [(ti ^ k).astype(jnp.uint32) for k in range(tensor_size)]
    zero = jnp.uint32(0)

    def zswap(x, k):
        return lax.ppermute(x, "tensor", [(i, i ^ k) for i in range(tensor_size)])

    def cswap(x, c):
        return lax.ppermute(x, "ctx", [(i, i ^ c) for i in range(ctx_size)])

    def own_order(x):
        blocked = x.reshape(tensor_size, -1, x.shape[1])
        picked = [
            lax.dynamic_slice(blocked, (i, zero, zero), (1,) + blocked.shape[1:]) for i in order_index
        ]
        return jnp.concatenate(picked, axis=0).reshape(x.shape)

    def exchange(blocks):
        return [blocks[0]] + [zswap(blocks[k], k) for k in others]

    def token_gather(x):
        return lax.optimization_barrier(jnp.concatenate([x] + [zswap(x, k) for k in others], axis=0))

    def token_sends(x):
        size = x.shape[0] // tensor_size
        return [x[k * size : (k + 1) * size].astype(bf16) for k in others]

    def token_swap(sends):
        return [zswap(x, k) for x, k in zip(sends, others)]

    def token_sum(own, got):
        for x in got:
            own = own + x.astype(f32)
        return own

    def key_swap(sent):
        return [cswap(x, c + 1) for c, x in enumerate(sent)]

    def key_sum(own, got):
        for x in got:
            own = own + x.astype(f32)
        return own.astype(bf16)

    gains = jnp.stack([norm_self, norm_cross, norm_ff], axis=1)
    gains = jnp.pad(gains, ((0, 0), (0, 128 - 3)))
    first = jnp.concatenate([w_query, w_key, w_value, gains], axis=1)
    turned = jnp.concatenate([w_out.T, c_query, c_out.T], axis=1)
    last_step = plane.size.bit_length() - 2

    one = plane.gather_start(first)
    for step in range(last_step):
        plane.gather_join(plane.gather_step(one, step), step)
    plane.gather_step(one, last_step)
    turned, one[0][0] = tie(turned, one[0][0])
    query_w, kv_w, gain_cols = plane.assemble(one, [head_cols, 2 * head_cols, 128])
    gain_rows = gain_cols.astype(f32).T
    gain_one, gain_two, gain_three = (gain_rows[i : i + 1] for i in range(3))

    turned_all = [turned] + [zswap(turned, k) for k in others]
    full = [t[:, i * head_cols : (i + 1) * head_cols] for i in range(3) for t in turned_all]
    second = jnp.concatenate([c_key, c_value] + full, axis=1)
    second, query_w = tie(second, query_w)
    two = plane.gather_start(second)
    for step in range(last_step):
        plane.gather_join(plane.gather_step(two, step), step)
    plane.gather_step(two, last_step)
    third = jnp.concatenate([w_gate, w_up, w_down.T], axis=1)
    third, two[0][0] = tie(third, two[0][0])
    ckv_w, out_wt, cquery_w, cout_wt = plane.assemble(two, [2 * head_cols] + [all_heads] * 3)
    three = plane.gather_start(third)
    for step in range(last_step):
        plane.gather_join(plane.gather_step(three, step), step)
    plane.gather_step(three, last_step)
    ff_w, down_wt = plane.assemble(three, [2 * ff_cols, ff_cols])

    blocks = jnp.arange(tensor_size, dtype=jnp.int32) ^ ti
    q_places = ci * tensor_size + blocks
    k_places = jnp.concatenate([(ci ^ c) * tensor_size + blocks for c in range(ctx_size)])

    def positions(places, size):
        return (places[:, None] * size + jnp.arange(size, dtype=jnp.int32)[None, :]).reshape(-1)

    live = (positions(q_places, chunk) < seq_len[0]).astype(f32)[:, None]
    self_mask = jnp.where(positions(k_places, chunk) < seq_len[0], 0.0, MASKED).astype(f32)[None]
    cross_mask = jnp.where(positions(k_places, enc_chunk) < enc_len[0], 0.0, MASKED).astype(f32)[None]

    steps = length // chunk
    buckets = lag_buckets(steps, chunk).reshape(-1)
    selector = jnp.asarray(np.eye(bucket_count, dtype=np.float32)[buckets])
    vectors = lax.dot_general(
        rel_table,
        selector,
        (((0,), (1,)), ((), ())),
        precision=lax.Precision.HIGHEST,
        preferred_element_type=f32,
    ).reshape(heads, steps, 2 * chunk)
    tiles = bias_tiles(vectors, chunk)
    places = (q_places, k_places)

    hidden_in = own_order(inputs[0])
    enc = own_order(encoded[0])
    hidden_in = hidden_in.astype(f32)
    normed_one, rescale_one, input_one = rms_norm(hidden_in, gain_one)
    kv_one = dot(input_one, kv_w).astype(bf16)
    kv_one = [kv_one] + [cswap(kv_one, c) for c in range(1, ctx_size)]
    query_one = dot(input_one, query_w).astype(bf16)
    attn_one, total_one = attend([query_one], kv_one, self_mask, heads, tensor_size, places, tiles)
    kv_two = dot(enc, ckv_w).astype(bf16)
    kv_two = [kv_two] + [cswap(kv_two, c) for c in range(1, ctx_size)]
    flat_one, hidden_one, input_two, query_two = stage_out(
        exchange(attn_one), out_wt, hidden_in, gain_two, cquery_w
    )
    query_two = exchange(query_two)
    attn_two, total_two = attend(query_two, kv_two, cross_mask, heads, tensor_size)
    flat_two, hidden_two, input_three, _ = stage_out(
        exchange(attn_two), cout_wt, hidden_one, gain_three, None
    )
    grad_out = own_order(cotangent[0]).astype(f32) * live
    grad_out_b = grad_out.astype(bf16)
    grad_ff = dot(grad_out_b, down_wt)
    input_three = token_gather(input_three)
    input_three, grad_ff = tie(input_three, grad_ff)
    pre = dot(input_three, ff_w)
    gate_pre, up_pre = pre[:, :ff_cols], pre[:, ff_cols:]
    gelu_value, gelu_slope = gelu_parts(gate_pre)
    ff_hidden = (gelu_value * up_pre).astype(bf16)
    ff_term = dot_nt(ff_hidden, down_wt)

    grad_pre = jnp.concatenate(
        [(grad_ff * up_pre * gelu_slope).astype(bf16), (grad_ff * gelu_value).astype(bf16)], axis=1
    )
    dn_three = dot_nt(grad_pre, ff_w)
    got_three = token_swap(token_sends(dn_three))
    packed = plane.pack([(input_three, grad_pre), (grad_out_b, ff_hidden)], shard_rows)
    got_three, packed = tie(got_three, packed)
    ff_scatter = Scatter(plane, packed).launch()
    grad_two, gain_grad_three, grad_two_b, *g_two = stage_back(
        dn_three, got_three, None, hidden_two, gain_three, grad_out, cout_wt, tensor_size, True
    )
    g_two = exchange(g_two)
    ff_scatter.absorb()
    g_two, ff_scatter.outgoing = tie(g_two, ff_scatter.outgoing)
    ff_scatter.launch()
    dq_two, own_two, sent_two, _ = attend_back(
        query_two, kv_two, cross_mask, total_two, g_two, heads, True
    )
    got_two = key_swap(sent_two)
    dq_two = exchange(dq_two)
    dq_two, ff_scatter.pending = tie(dq_two, ff_scatter.pending)
    ff_scatter.absorb()
    dq_two, ff_scatter.outgoing = tie(dq_two, ff_scatter.outgoing)
    ff_scatter.launch()
    grad_one, flat_dq_two, gain_grad_two, grad_one_b, *g_one = stage_back(
        dq_two[0], dq_two[1:], cquery_w, hidden_one, gain_two, grad_two, out_wt, tensor_size, True
    )
    g_one = exchange(g_one)
    kv_grad_two = key_sum(own_two, got_two)
    packed = plane.pack(
        [
            (grad_one_b, flat_one),
            (grad_two_b, flat_two),
            (input_two, flat_dq_two),
            (enc, kv_grad_two),
        ],
        shard_rows,
    )
    enc_partial = dot_nt(kv_grad_two, ckv_w)
    enc_sends = token_sends(enc_partial)
    ff_sends = token_sends(ff_term)
    g_one, (packed, enc_sends, ff_sends, ff_scatter.pending) = tie(
        g_one, (packed, enc_sends, ff_sends, ff_scatter.pending)
    )
    ff_sum = ff_scatter.absorb().finish()
    mid_scatter = Scatter(plane, packed).launch()
    enc_got = token_swap(enc_sends)
    ff_got = token_swap(ff_sends)
    dq_one, own_one, sent_one, lag_sums = attend_back(
        [query_one], kv_one, self_mask, total_one, g_one, heads, False, places, tiles
    )
    dq_one = dq_one[0]
    got_one = key_swap(sent_one)
    mid_scatter.absorb()
    layer_rows = (hidden_two + token_sum(ff_term[:chunk], ff_got)).astype(bf16)
    enc_sum = token_sum(enc_partial[:enc_chunk], enc_got).astype(bf16)
    side_rows = jnp.concatenate([layer_rows, enc_sum], axis=0)
    got_one, (mid_scatter.outgoing, side_rows) = tie(got_one, (mid_scatter.outgoing, side_rows))
    mid_scatter.launch()
    side = [side_rows] + [zswap(side_rows, k) for k in others]
    kv_grad_one = key_sum(own_one, got_one)
    dn_one = dot_nt(kv_grad_one, kv_w) + dot_nt(dq_one, query_w)
    got_dn = token_swap(token_sends(dn_one))
    gain_grad_one = jnp.sum(dn_one * normed_one, axis=0, keepdims=True)
    packed = plane.pack([(input_one, kv_grad_one), (input_one, dq_one)], shard_rows)
    table_term = lax.dot_general(
        selector,
        lag_sums.reshape(heads, -1),
        (((0,), (1,)), ((), ())),
        precision=lax.Precision.HIGHEST,
        preferred_element_type=f32,
    )
    table_row = jnp.pad(table_term.reshape(1, -1), ((0, 0), (0, width - bucket_count * heads)))
    small = jnp.concatenate([gain_grad_one, gain_grad_two, gain_grad_three, table_row], axis=0)
    got_dn, (packed, small, mid_scatter.pending) = tie(
        got_dn, (packed, small, mid_scatter.pending)
    )
    self_scatter = Scatter(plane, packed).launch()
    mid_scatter.absorb()
    small = small + plane.swap(small, plane.near)
    (grad_rows,) = stage_back(
        dn_one, got_dn, None, hidden_in, gain_one, grad_one, None, tensor_size, False
    )
    grad_all = [grad_rows] + [zswap(grad_rows, k) for k in others]
    for bit in plane.orders[0]:
        small = small + plane.swap(small, bit)
    table_row = small[3, : bucket_count * heads]
    small = small[:3]
    bit = 1
    while bit < tensor_size:
        small = small + zswap(small, bit)
        bit *= 2
    small = lax.dynamic_slice_in_dim(small, plane.me * shard_rows, shard_rows, 1)
    mid_sum = mid_scatter.finish()

    full_grad = mid_sum[:, : 3 * all_heads].reshape(shard_rows, 3, tensor_size, head_cols)
    full_sum = full_grad[:, :, 0].reshape(shard_rows, -1)
    for k in others:
        sent = full_grad[:, :, k].reshape(shard_rows, -1).astype(bf16)
        full_sum = full_sum + zswap(sent, k).astype(f32)
    self_sum = self_scatter.absorb().finish()

    side = lax.optimization_barrier(side)
    layer_out = own_order(jnp.concatenate([x[:chunk] for x in side], axis=0))
    grad_encoded = own_order(jnp.concatenate([x[chunk:] for x in side], axis=0)).astype(f32)
    grad_all = lax.optimization_barrier(jnp.concatenate(grad_all, axis=0))
    grad_inputs = own_order(grad_all).astype(f32)
    cols = lambda x, lo, n: x[:, lo : lo + n]
    return (
        layer_out[None],
        grad_inputs[None],
        grad_encoded[None],
        small[0],
        cols(self_sum, 2 * head_cols, head_cols),
        cols(self_sum, 0, head_cols),
        cols(self_sum, head_cols, head_cols),
        cols(full_sum, 0, head_cols).T,
        table_row.reshape(bucket_count, heads),
        small[1],
        cols(full_sum, 2 * head_cols, head_cols),
        cols(mid_sum, 3 * all_heads, head_cols),
        cols(mid_sum, 3 * all_heads + head_cols, head_cols),
        cols(full_sum, head_cols, head_cols).T,
        small[2],
        cols(ff_sum, 0, ff_cols),
        cols(ff_sum, ff_cols, ff_cols),
        cols(ff_sum, 2 * ff_cols, ff_cols).T,
    )


def solution(mesh):
    rows_in = P(("dp", "ctx"), "tensor")
    rows_out = P("tensor", ("dp", "ctx"))
    gain = P(("dp", "ctx"))
    token = P("dp", "ctx", None)
    table = P(None, "tensor")
    return jax.shard_map(
        shards,
        mesh=mesh,
        in_specs=(
            token,
            token,
            P("dp"),
            P("dp"),
            gain,
            rows_in,
            rows_in,
            rows_in,
            rows_out,
            table,
            gain,
            rows_in,
            rows_in,
            rows_in,
            rows_out,
            gain,
            rows_in,
            rows_in,
            rows_out,
            token,
        ),
        out_specs=(
            token,
            token,
            token,
            gain,
            rows_in,
            rows_in,
            rows_in,
            rows_out,
            table,
            gain,
            rows_in,
            rows_in,
            rows_in,
            rows_out,
            gain,
            rows_in,
            rows_in,
            rows_out,
        ),
        check_vma=False,
    )
```
